32 devices in a mesh: section: 4 (over y, x), dp: 8 (over z, core).
Axes of the slice: x: 2, y: 2, z: 4, core: 2. Of those that a mesh axis runs over, the one named last changes fastest.
Arguments:
- inputs: bfloat16 [1024, 1600], P('dp'), may hold values from -6 to 6
- targets: bfloat16 [1024, 1600], P('dp'), may hold values from -6 to 6
- weight_in: bfloat16 [4, 1600, 3200], P('section'), may hold values from -0.15625 to 0.15625
- hidden_bias: float32 [4, 3200], P('section'), may hold values from -3 to 3
- norm_gain: float32 [4, 1600], P('section'), may hold values from 0.5 to 1.5
- weight_out: bfloat16 [4, 3200, 1600], P('section'), may hold values from -0.109375 to 0.109375
- current: float32 [4, 3200, 1600], P('section', 'dp')
- previous: float32 [4, 3200, 1600], P('section', 'dp')
- older_basis: float32 [2, 4, 3200, 1600], P(None, 'section', 'dp')
- beta_before: float32 [1], replicated, may hold values from 1 to 4
Outputs:
- next_vector: float32 [4, 3200, 1600], P('section', 'dp')
- tridiagonal_entries: float32 [2], replicated
The draws below stay inside these ranges and needn't reach their ends.
All inputs are finite; a program needn't handle non-finite values.
Results may differ from the reference program's by a relative error of at most 0.012.
Values may be sent and summed in bfloat16 or wider, within the bound.
No kernel may reach another device: no remote copies, remote signals or barrier semaphores. Data moves between devices by JAX's collectives and lax.ppermute only.
A program may use at most 192 MiB of HBM per device.

```python
import math
from functools import partial
import jax
import jax.numpy as jnp
from jax import lax

D = 1600
FF = 3200
KEEP = 2
SECTIONS = 4
ROWS = 1024


def spread_vectors(key, members):
    subkeys = jax.random.split(key, 4)
    normal_part = jax.random.normal(subkeys[0], (members, SECTIONS, FF, D), jnp.float32)
    rise_along = jnp.exp(jnp.log(3.0) * jnp.arange(FF, dtype=jnp.float32) / FF)[:, None]
    section_scale = jnp.exp(jnp.log(2.0) * jax.random.uniform(subkeys[3], (members, SECTIONS, 1, 1), jnp.float32))
    return normal_part * rise_along * section_scale


def lanczos_vectors(key):
    raw_draw = spread_vectors(jax.random.fold_in(key, 7), KEEP + 2)
    members = []
    for member in range(KEEP + 2):
        vector = raw_draw[member]
        for passes in range(2):
            for earlier in members:
                vector = vector - jnp.mean(vector * earlier) * earlier
        vector = vector / jnp.sqrt(jnp.mean(vector * vector))
        members.append(vector)
    correlation = jax.random.uniform(jax.random.fold_in(key, 8), (KEEP,), jnp.float32, 0.3, 0.6)
    drifted = members[KEEP]
    for member in range(KEEP):
        drifted = drifted + correlation[member] * members[member]
    drifted = drifted / jnp.sqrt(jnp.mean(drifted * drifted))
    return (jnp.stack(members[:KEEP]), drifted, members[KEEP + 1])


def draw_current(key, part):
    return lanczos_vectors(key)[2]


def draw_previous(key, part):
    return lanczos_vectors(key)[1]


def draw_older_basis(key, part):
    return lanczos_vectors(key)[0]


def block_scale(own_key, extent, pieces, least, top_value):
    level, own = 1.0, jax.random.fold_in(own_key, 6)
    for axis_at, shards_of in pieces:
        heights = jnp.exp(jax.random.uniform(jax.random.fold_in(own, axis_at), (shards_of,), jnp.float32, least / len(pieces), top_value / len(pieces)))
        level = level * jnp.repeat(heights, extent[axis_at] // shards_of).reshape([-1 if axis == axis_at else 1 for axis in range(len(extent))])
    return level


def noise(rng, dims, deviation, limit, cuts=(), held_as=jnp.bfloat16):
    drawn = jax.random.normal(rng, dims, jnp.float32) * deviation
    if len(cuts) > 0:
        drawn = block_scale(rng, dims, cuts, -0.22, 0.18) * drawn
    return jnp.clip(drawn, min=-limit, max=limit).astype(held_as)


def setup_inputs(seed: int = 0) -> dict:
    key_of = jax.random.split(jax.random.key(seed), 11)
    return {
        "inputs": noise(key_of[0], (ROWS, D), 1.0, 6.0, ((0, 8),)),
        "targets": noise(key_of[1], (ROWS, D), 1.0, 6.0, ((0, 8),)),
        "weight_in": noise(key_of[2], (SECTIONS, D, FF), D ** -0.5, 0.15625, ((0, 4),)),
        "hidden_bias": noise(key_of[3], (SECTIONS, FF), 0.5, 3.0, ((0, 4),), jnp.float32),
        "norm_gain": jnp.clip(1.0 + 0.1 * jax.random.normal(key_of[4], (SECTIONS, D), jnp.float32), 0.5, 1.5),
        "weight_out": noise(key_of[5], (SECTIONS, FF, D), FF ** -0.5, 0.109375, ((0, 4),)),
        "current": draw_current(jax.random.fold_in(key_of[10], 71), 0),
        "previous": draw_previous(jax.random.fold_in(key_of[10], 71), 0),
        "older_basis": draw_older_basis(jax.random.fold_in(key_of[10], 71), 0),
        "beta_before": jnp.clip(jnp.exp(jax.random.uniform(key_of[9], (1,), jnp.float32, math.log(1.0), math.log(4.0))), 1.0, 4.0),
    }


def gelu_tanh(values):
    return jax.nn.gelu(values, approximate=True)

def gelu_slope(values):
    return jax.jvp(gelu_tanh, (values,), (jnp.ones_like(values),))[1]

def gelu_bend(values):
    return jax.jvp(gelu_slope, (values,), (jnp.ones_like(values),))[1]

def normalize(values, gain_row):
    mean_value = lax.optimization_barrier(jnp.mean(values, axis=-1, keepdims=True))
    centered = values - mean_value
    variance = lax.optimization_barrier(jnp.mean(centered * centered, axis=-1, keepdims=True))
    return centered * lax.rsqrt(variance + 1e-05) * gain_row

def times_transposed(left, right):
    return lax.dot_general(left, right, (((1,), (1,)), ((), ())), preferred_element_type=jnp.float32)

def contract_rows(left, right):
    return lax.dot_general(left, right, (((0,), (0,)), ((), ())), preferred_element_type=jnp.float32)

def layer_inner(rows_in, tangent_in, weight_in, bias_row, gain_row):
    rows_float = rows_in.astype(jnp.float32)
    tangent_float = tangent_in.astype(jnp.float32)
    normed, normed_dot = jax.jvp(partial(normalize, gain_row=gain_row), (rows_float,), (tangent_float,))
    preact = jnp.dot(normed.astype(jnp.bfloat16), weight_in, preferred_element_type=jnp.float32) + bias_row
    preact_dot = jnp.dot(normed_dot.astype(jnp.bfloat16), weight_in, preferred_element_type=jnp.float32)
    hidden = gelu_tanh(preact).astype(jnp.bfloat16)
    hidden_dot = (gelu_slope(preact) * preact_dot).astype(jnp.bfloat16)
    return (rows_float, tangent_float, preact, preact_dot, hidden, hidden_dot)

def layer_forward(rows_in, tangent_in, weight_in, bias_row, gain_row, weight_out, direction):
    rows_float, tangent_float, preact, preact_dot, hidden, hidden_dot = layer_inner(rows_in, tangent_in, weight_in, bias_row, gain_row)
    rows_out = rows_float + jnp.dot(hidden, weight_out, preferred_element_type=jnp.float32)
    tangent_out = tangent_float + jnp.dot(hidden_dot, weight_out, preferred_element_type=jnp.float32)
    tangent_out = tangent_out + jnp.dot(hidden, direction, preferred_element_type=jnp.float32)
    return (rows_out.astype(jnp.bfloat16), tangent_out.astype(jnp.bfloat16))

def layer_backward(rows_in, tangent_in, grad_out, grad_dot_out, weight_in, bias_row, gain_row, weight_out, direction):
    rows_float, tangent_float, preact, preact_dot, hidden, hidden_dot = layer_inner(rows_in, tangent_in, weight_in, bias_row, gain_row)
    back_hidden = times_transposed(grad_out, weight_out)
    back_hidden_dot = times_transposed(grad_dot_out, weight_out) + times_transposed(grad_out, direction)
    slope = gelu_slope(preact)
    pre_grad = (slope * back_hidden).astype(jnp.bfloat16)
    pre_grad_dot = (gelu_bend(preact) * preact_dot * back_hidden + slope * back_hidden_dot).astype(jnp.bfloat16)
    norm_grad = times_transposed(pre_grad, weight_in)
    norm_grad_dot = times_transposed(pre_grad_dot, weight_in)

    def pull_back(values, cotangent):
        return jax.vjp(partial(normalize, gain_row=gain_row), values)[1](cotangent)[0]
    grad_in, grad_in_dot = jax.jvp(pull_back, (rows_float, norm_grad), (tangent_float, norm_grad_dot))
    grad_next = (grad_out.astype(jnp.float32) + grad_in).astype(jnp.bfloat16)
    grad_dot_next = (grad_dot_out.astype(jnp.float32) + grad_in_dot).astype(jnp.bfloat16)
    return (grad_next, grad_dot_next, hidden, hidden_dot)

def reference(inputs, targets, weight_in, hidden_bias, norm_gain, weight_out, current, previous, older_basis, beta_before):
    levels = weight_in.shape[0]
    row_count = float(inputs.shape[0])
    rows_now = inputs
    tangent_now = jnp.zeros_like(inputs)
    saved = []
    for level in range(levels):
        direction = current[level].astype(jnp.bfloat16)
        saved.append((rows_now, tangent_now))
        rows_now, tangent_now = layer_forward(rows_now, tangent_now, weight_in[level], hidden_bias[level], norm_gain[level], weight_out[level], direction)
    grad_now = ((rows_now.astype(jnp.float32) - targets.astype(jnp.float32)) / row_count).astype(jnp.bfloat16)
    grad_dot_now = (tangent_now.astype(jnp.float32) / row_count).astype(jnp.bfloat16)
    products = [None] * levels
    for level in reversed(range(levels)):
        direction = current[level].astype(jnp.bfloat16)
        grad_next, grad_dot_next, hidden, hidden_dot = layer_backward(saved[level][0], saved[level][1], grad_now, grad_dot_now, weight_in[level], hidden_bias[level], norm_gain[level], weight_out[level], direction)
        products[level] = contract_rows(hidden_dot, grad_now) + contract_rows(hidden, grad_dot_now)
        grad_now, grad_dot_now = (grad_next, grad_dot_next)
    hvp = jnp.stack(products)
    entry_count = float(hvp.size)
    start_vec = hvp - beta_before[0] * previous
    alpha_value = jnp.sum(start_vec * current) / entry_count
    first_resid = start_vec - alpha_value * current
    basis = jnp.concatenate([older_basis, previous[None], current[None]], axis=0)
    coeffs = lax.optimization_barrier(jnp.sum(basis * first_resid[None], axis=(1, 2, 3))) / entry_count
    second = first_resid - lax.optimization_barrier(jnp.sum(coeffs[:, None, None, None] * basis, axis=0))
    beta_value = jnp.sqrt(jnp.sum(second * second) / entry_count + 1e-06)
    return (second / beta_value, jnp.stack([alpha_value, beta_value]))
```

```python
import math

import jax
import jax.numpy as jnp
from jax import lax
from jax.experimental import pallas as pl
from jax.experimental.pallas import tpu as pltpu
from jax.sharding import PartitionSpec as P

F32 = jnp.float32
BF16 = jnp.bfloat16
PIECES = 2
UNROLL = False
ROOT = 0.7978845608028654
CUBE = 0.044715
EPS = 1e-05


def chunk_of(width):
    for parts in range(1, width + 1):
        if width % parts == 0 and width // parts <= 640 and (width // parts) % 128 == 0:
            return width // parts
    return width


def gelu_parts(v):
    square = v * v
    t = jnp.tanh(ROOT * v * (1.0 + CUBE * square))
    return square, t


def gelu_value(v):
    _, t = gelu_parts(v)
    return 0.5 * v * (1.0 + t)


def gelu_slope(v):
    square, t = gelu_parts(v)
    rise = ROOT * (1.0 + 3.0 * CUBE * square)
    return 0.5 * (1.0 + t) + 0.5 * v * (1.0 - t * t) * rise


def gelu_slope_bend(v):
    square, t = gelu_parts(v)
    rise = ROOT * (1.0 + 3.0 * CUBE * square)
    fall = 1.0 - t * t
    slope = 0.5 * (1.0 + t) + 0.5 * v * fall * rise
    bend = fall * (rise + v * (3.0 * ROOT * CUBE * v - t * rise * rise))
    return slope, bend


def mean_of(v):
    return jnp.mean(v, axis=-1, keepdims=True)


def standardize(x):
    centered = x - mean_of(x)
    scale = lax.rsqrt(mean_of(centered * centered) + EPS)
    return centered * scale, scale


def dot_nn(a, b):
    return lax.dot_general(a, b, (((1,), (0,)), ((), ())), preferred_element_type=F32)


def dot_nt(a, b):
    return lax.dot_general(a, b, (((1,), (1,)), ((), ())), preferred_element_type=F32)


def xor_pairs(count, bit):
    return [(i, i ^ bit) for i in range(count)]


class Stage:
    def __init__(self, rows, width, hidden, where, w_in, w_out_t, gain):
        self.rows, self.width, self.hidden = rows, width, hidden
        self.chunk = chunk_of(hidden)
        self.parts = hidden // self.chunk
        self.where, self.w_in, self.w_out_t, self.gain = where, w_in, w_out_t, gain
        self.token = gain
        self.dirs = None

    def accumulator(self):
        return [pltpu.VMEM((self.rows, self.width), F32)]

    def sweep(self, step):
        if UNROLL:
            for j in range(self.parts):
                step(j, slice(j * self.chunk, (j + 1) * self.chunk))
            return

        def run(j, carry):
            step(j, pl.ds(pl.multiple_of(j * self.chunk, self.chunk), self.chunk))
            return carry

        lax.fori_loop(0, self.parts, run, 0)

    def call(self, kernel, arrays, outs, scratch, aliases=None, heavy=True, load=False, kept=(), limit=10):
        count = len(arrays)
        spec = []
        for one in arrays:
            if one is self.dirs:
                spec.append(pl.BlockSpec(memory_space=pltpu.VMEM))
            elif one is self.w_in or one is self.w_out_t:
                spec.append(pl.BlockSpec(memory_space=pl.ANY if load else pltpu.VMEM))
            elif one.dtype == jnp.int32:
                spec.append(pl.BlockSpec(memory_space=pltpu.SMEM))
            elif one.ndim == 2 and one.shape[0] == 1:
                spec.append(pl.BlockSpec(memory_space=pltpu.VMEM))
            elif one.ndim == 3 or one.dtype == F32:
                spec.append(pl.BlockSpec(memory_space=pltpu.HBM))
            else:
                spec.append(pl.BlockSpec(memory_space=pl.ANY))

        def wrapped(*refs):
            kernel(*refs[:count], *refs[count + 1 :])

        kept = [pltpu.VMEM(shape, dtype) for shape, dtype in kept]
        out_spec = [
            pl.BlockSpec(memory_space=pltpu.HBM if len(one.shape) == 3 or one.dtype == F32 else pl.ANY)
            for one in outs
        ]
        out_spec += [pl.BlockSpec(memory_space=pltpu.VMEM) for _ in kept]
        result = pl.pallas_call(
            wrapped,
            out_shape=outs + kept,
            in_specs=spec + [pl.BlockSpec(memory_space=pl.ANY)],
            out_specs=out_spec,
            scratch_shapes=scratch,
            input_output_aliases=aliases or {},
            compiler_params=pltpu.CompilerParams(vmem_limit_bytes=limit * 2**20),
            cost_estimate=pl.CostEstimate(
                flops=4 * self.rows * self.width * self.hidden if heavy else 1000,
                bytes_accessed=4 * self.width * self.hidden if heavy else 1000,
                transcendentals=0,
            ),
        )
        result = list(result(*arrays, self.token))
        self.token = result[0]
        return result


def fetch(copies):
    for one in copies:
        one.start()
    for one in copies:
        one.wait()


def struct(shape, dtype):
    return jax.ShapeDtypeStruct(shape, dtype)


def vmem(*shape, dtype=BF16):
    return pltpu.VMEM(shape, dtype)


def sems(count):
    return pltpu.SemaphoreType.DMA((count,))


def pick(section, pairs):
    live, piece = False, 0
    for s, k in pairs:
        hit = section == s
        live = jnp.logical_or(live, hit)
        piece = piece + jnp.where(hit, k, 0)
    return live, piece


def stage_forward(st, pairs, inputs, arrived, bias, state, extra=()):
    r, w, h = st.rows, st.width, st.hidden
    held = 5 if state else len(extra)
    load = not state
    half = h // 2

    def kernel(*refs):
        where, inp, arr, bias_r, gain, win, wout = refs[:7]
        send, x_st, pre_st, hid_st, mine_st, theirs_st = refs[7 + held : 13 + held]
        rest = refs[13 + held :]
        if load:
            win_v, wout_v, rest = rest[0], rest[1], rest[2:]
        acc, sem, xb, preb, hidb, sendb, halfb = rest[:7]
        section = where[0]
        live, k = pick(section, pairs)
        if load:
            wsem = rest[7]

            def flow(row, j):
                cols = pl.ds(pl.multiple_of(j * st.chunk, st.chunk), st.chunk)
                source, target = ((win, win_v), (wout, wout_v))[row]
                return pltpu.make_async_copy(source.at[:, cols], target.at[:, cols], wsem.at[row, j])

            for j in range(st.parts):
                flow(0, j).start()
                flow(1, j).start()

            @pl.when(jnp.logical_not(live))
            def _():
                for j in range(st.parts):
                    flow(0, j).wait()
                    flow(1, j).wait()

        in_w, out_w = (win_v, wout_v) if load else (win, wout)

        @pl.when(live)
        def _():
            own = pltpu.make_async_copy(inp.at[k], xb, sem.at[0])
            other = pltpu.make_async_copy(arr, xb, sem.at[0])

            @pl.when(section == 0)
            def _():
                own.start()

            @pl.when(section != 0)
            def _():
                other.start()

            other.wait()
            x = xb[...].astype(F32)
            x_hat, _ = standardize(x)
            normed = (x_hat * gain[...]).astype(BF16)
            acc[...] = x

            def step(j, cols):
                if load:
                    flow(0, j).wait()
                pre = dot_nn(normed, in_w[:, cols]) + bias_r[:, cols]
                preb[:, cols] = pre
                hid = gelu_value(pre).astype(BF16)
                hidb[:, cols] = hid
                if load:
                    flow(1, j).wait()
                acc[...] += dot_nt(hid, out_w[:, cols])

            st.sweep(step)
            sendb[...] = acc[...].astype(BF16)
            halfb[0] = hidb[:, :half]
            halfb[1] = hidb[:, half:]
            upper = where[1]
            fetch(
                [
                    pltpu.make_async_copy(sendb, send, sem.at[1]),
                    pltpu.make_async_copy(xb, x_st.at[k], sem.at[2]),
                    pltpu.make_async_copy(preb, pre_st.at[k], sem.at[3]),
                    pltpu.make_async_copy(hidb, hid_st.at[k], sem.at[4]),
                    pltpu.make_async_copy(halfb.at[upper], mine_st.at[k], sem.at[5]),
                    pltpu.make_async_copy(halfb.at[1 - upper], theirs_st.at[k], sem.at[6]),
                ]
            )

    outs = [
        struct((r, w), BF16),
        struct((PIECES, r, w), BF16),
        struct((PIECES, r, h), F32),
        struct((PIECES, r, h), BF16),
        struct((PIECES, r, half), BF16),
        struct((PIECES, r, half), BF16),
    ]
    scratch = st.accumulator() + [sems(7), vmem(r, w), vmem(r, h, dtype=F32), vmem(r, h), vmem(r, w)]
    scratch.append(vmem(2, r, half))
    if load:
        scratch.append(pltpu.SemaphoreType.DMA((2, st.parts)))
    arrays = [st.where, inputs, arrived, bias, st.gain, st.w_in, st.w_out_t] + (state[1:] if state else [])
    aliases = {7 + i: 1 + i for i in range(held)} if state else {}
    if not load:
        return st.call(kernel, arrays, outs, scratch, aliases)
    kept = [((w, h), BF16)] * 2
    result = st.call(kernel, arrays + list(extra), outs, scratch, aliases, load=True, kept=kept, limit=42)
    st.w_in, st.w_out_t = result[-2:]
    return result[:-2]


def stage_tangent(st, pairs, from_first, arrived, u_mine, u_recv, forward, state):
    r, w, h = st.rows, st.width, st.hidden
    held = 3 if state else 0

    def kernel(*refs):
        where, arr0, arr, um, ur0, ur1, gain, win, wout, x_st, pre_st = refs[:11]
        send, tan_st, pd_st, hd_st, acc, sem = refs[11 + held : 17 + held]
        tb, xb, preb, pdb, hdb, umb, urb, sendb = refs[17 + held :]
        section = where[0]
        live, k = pick(section, pairs)

        if not state:

            @pl.when(section == 0)
            def _():
                hdb[...] = jnp.zeros_like(hdb)
                fetch([pltpu.make_async_copy(hdb, hd_st.at[i], sem.at[i]) for i in range(PIECES)])

        @pl.when(live)
        def _():
            came0 = pltpu.make_async_copy(arr0, tb, sem.at[2])
            came = pltpu.make_async_copy(arr, tb, sem.at[2])
            back0 = pltpu.make_async_copy(ur0, urb, sem.at[1])
            back1 = pltpu.make_async_copy(ur1, urb, sem.at[1])
            mine = pltpu.make_async_copy(um.at[k], umb, sem.at[0])
            takes = [
                pltpu.make_async_copy(x_st.at[k], xb, sem.at[3]),
                pltpu.make_async_copy(pre_st.at[k], preb, sem.at[4]),
            ]

            @pl.when(section == 1)
            def _():
                came0.start()

            @pl.when(section != 1)
            def _():
                came.start()

            for one in takes:
                one.start()
            mine.start()

            @pl.when(k == 0)
            def _():
                back0.start()

            @pl.when(k != 0)
            def _():
                back1.start()

            came.wait()
            for one in takes:
                one.wait()
            tan = tb[...].astype(F32)
            x_hat, scale = standardize(xb[...].astype(F32))
            shift = tan - mean_of(tan)
            normed_dot = (gain[...] * scale * (shift - x_hat * mean_of(x_hat * shift))).astype(BF16)
            acc[...] = tan

            def step(j, cols):
                pre_dot = dot_nn(normed_dot, win[:, cols])
                pdb[:, cols] = pre_dot
                hid_dot = (gelu_slope(preb[:, cols]) * pre_dot).astype(BF16)
                hdb[:, cols] = hid_dot
                acc[...] += dot_nt(hid_dot, wout[:, cols])

            st.sweep(step)
            mine.wait()
            back0.wait()
            sendb[...] = (acc[...] + umb[...] + urb[...].astype(F32)).astype(BF16)
            fetch(
                [
                    pltpu.make_async_copy(sendb, send, sem.at[5]),
                    pltpu.make_async_copy(tb, tan_st.at[k], sem.at[6]),
                    pltpu.make_async_copy(pdb, pd_st.at[k], sem.at[7]),
                    pltpu.make_async_copy(hdb, hd_st.at[k], sem.at[8]),
                ]
            )

    outs = [
        struct((r, w), BF16),
        struct((PIECES, r, w), BF16),
        struct((PIECES, r, h), F32),
        struct((PIECES, r, h), BF16),
    ]
    scratch = st.accumulator() + [
        sems(9), vmem(r, w), vmem(r, w), vmem(r, h, dtype=F32), vmem(r, h, dtype=F32), vmem(r, h),
        vmem(r, w, dtype=F32), vmem(r, w), vmem(r, w),
    ]
    arrays = [st.where, from_first, arrived, u_mine, u_recv[0], u_recv[1], st.gain, st.w_in, st.w_out_t]
    arrays += [forward[1], forward[2]] + (state[1:] if state else [])
    aliases = {11 + i: 1 + i for i in range(held)}
    return st.call(kernel, arrays, outs, scratch, aliases)


def stage_gradient(st, pairs, last, row_count, arrived, top, goal, forward, state):
    r, w, h = st.rows, st.width, st.hidden
    held = 1 if state else 0

    def kernel(*refs):
        where, arr, top_r, goal_r, gain, win, wout, x_st, pre_st = refs[:9]
        send, g_st, feed, back_o, ng_o, acc, sem = refs[9 + held : 16 + held]
        gb, tb, xb, preb, backb, sendb = refs[16 + held :]
        section = where[0]
        live, k = pick(section, pairs)

        if not state:

            @pl.when(section == 0)
            def _():
                gb[...] = jnp.zeros_like(gb)
                fetch([pltpu.make_async_copy(gb, g_st.at[i], sem.at[i]) for i in range(PIECES)])

        @pl.when(live)
        def _():
            takes = [
                pltpu.make_async_copy(x_st.at[k], xb, sem.at[2]),
                pltpu.make_async_copy(pre_st.at[k], preb, sem.at[3]),
            ]
            grad_in = pltpu.make_async_copy(arr, gb, sem.at[0])
            top_in = pltpu.make_async_copy(top_r, gb, sem.at[0])
            goal_in = pltpu.make_async_copy(goal_r.at[k], tb, sem.at[1])

            @pl.when(section == last)
            def _():
                top_in.start()
                goal_in.start()

            @pl.when(section != last)
            def _():
                grad_in.start()

            for one in takes:
                one.start()
            grad_in.wait()

            @pl.when(section == last)
            def _():
                goal_in.wait()
                gap = gb[...].astype(F32) - tb[...].astype(F32)
                gb[...] = (gap / row_count).astype(BF16)

            for one in takes:
                one.wait()
            grad = gb[...]
            x_hat, scale = standardize(xb[...].astype(F32))
            acc[...] = jnp.zeros_like(acc)

            def step(j, cols):
                back = dot_nn(grad, wout[:, cols])
                backb[:, cols] = back
                pre_grad = (gelu_slope(preb[:, cols]) * back).astype(BF16)
                acc[...] += dot_nt(pre_grad, win[:, cols])

            st.sweep(step)
            h_grad = acc[...] * gain[...]
            move = scale * (h_grad - mean_of(h_grad) - x_hat * mean_of(h_grad * x_hat))
            sendb[...] = (grad.astype(F32) + move).astype(BF16)
            fetch(
                [
                    pltpu.make_async_copy(sendb, send, sem.at[4]),
                    pltpu.make_async_copy(gb, g_st.at[k], sem.at[5]),
                    pltpu.make_async_copy(backb, back_o, sem.at[6]),
                    pltpu.make_async_copy(acc, ng_o, sem.at[7]),
                    pltpu.make_async_copy(gb, feed, sem.at[8]),
                ]
            )

    outs = [
        struct((r, w), BF16),
        struct((PIECES, r, w), BF16),
        struct((r, w), BF16),
        struct((r, h), F32),
        struct((r, w), F32),
    ]
    scratch = st.accumulator() + [
        sems(9), vmem(r, w), vmem(r, w), vmem(r, w), vmem(r, h, dtype=F32), vmem(r, h, dtype=F32), vmem(r, w),
    ]
    arrays = [st.where, arrived, top, goal, st.gain, st.w_in, st.w_out_t, forward[1], forward[2]]
    arrays += state[1:2] if state else []
    return st.call(kernel, arrays, outs, scratch, {9: 1} if state else {})


def stage_direction(st, pieces, theirs, mine):
    r, w = st.rows, st.width
    offsets = sorted(pieces)
    half = mine.shape[2]
    block = half // len(offsets)

    def kernel(where, theirs_r, mine_r, *refs):
        parts, refs = refs[: len(offsets)], refs[len(offsets) :]
        backs, u_mine, dirs, fb, ub, bb, sem, psem = refs[:PIECES], *refs[PIECES:]
        low = where[3]
        copies = []
        for i, offset in enumerate(offsets):
            place = 0
            if len(offsets) > 1:
                place = pl.multiple_of((low ^ offset) * block, math.gcd(block, 16))
            copies.append(pltpu.make_async_copy(parts[i], dirs.at[pl.ds(place, block), :], psem.at[i]))
        copies.append(pltpu.make_async_copy(theirs_r, fb.at[pl.ds(0, PIECES)], sem.at[0]))
        copies.append(pltpu.make_async_copy(mine_r, fb.at[pl.ds(PIECES, PIECES)], sem.at[1]))
        fetch(copies)
        both = dot_nn(fb[...].reshape(2 * PIECES * r, half), dirs[...])
        for i in range(PIECES):
            bb[i] = both[i * r : (i + 1) * r].astype(BF16)
            ub[i] = both[(PIECES + i) * r : (PIECES + i + 1) * r]
        copies = [pltpu.make_async_copy(bb.at[i], backs[i], psem.at[i]) for i in range(PIECES)]
        fetch(copies + [pltpu.make_async_copy(ub, u_mine, sem.at[0])])

    outs = [struct((r, w), BF16) for _ in range(PIECES)] + [struct((PIECES, r, w), F32)]
    scratch = [
        vmem(2 * PIECES, r, half),
        vmem(PIECES, r, w, dtype=F32),
        vmem(PIECES, r, w),
        sems(2),
        sems(max(PIECES, len(offsets))),
    ]
    arrays = [st.where, theirs, mine] + [pieces[offset] for offset in offsets]
    result = st.call(kernel, arrays, outs, scratch, heavy=False, kept=[((half, w), BF16)], limit=12)
    st.dirs = result[-1]
    return result[:PIECES], result[PIECES]


def stage_first(st, u_mine, u_recv, piece):
    r, w = st.rows, st.width

    def kernel(where, um, ur, send, a, b, c, sem):
        @pl.when(where[0] == 0)
        def _():
            fetch([pltpu.make_async_copy(um.at[piece], a, sem.at[0]), pltpu.make_async_copy(ur, b, sem.at[1])])
            c[...] = (a[...] + b[...].astype(F32)).astype(BF16)
            fetch([pltpu.make_async_copy(c, send, sem.at[0])])

    scratch = [vmem(r, w, dtype=F32), vmem(r, w), vmem(r, w), sems(2)]
    return st.call(kernel, [st.where, u_mine, u_recv], [struct((r, w), BF16)], scratch, heavy=False)[0]


def stage_split(st, sources, replicas):
    r, h = st.rows, st.hidden
    share = h // replicas
    span = PIECES * r
    count = len(sources)

    def kernel(where, *refs):
        srcs, refs = refs[:count], refs[count:]
        outs, (sb, blocks, sem) = refs[: replicas // 2], refs[replicas // 2 :]
        me = where[2]
        fetch([pltpu.make_async_copy(one, sb.at[i], sem.at[i]) for i, one in enumerate(srcs)])
        for i in range(replicas):
            for j in range(count):
                for k in range(PIECES):
                    at = j * span + k * r
                    blocks[i, at : at + r, :] = sb[j, k, :, i * share : (i + 1) * share]
        copies = []
        for q in range(replicas // 2):
            for side in range(2):
                copies.append(
                    pltpu.make_async_copy(blocks.at[me ^ (2 * q + side)], outs[q].at[side], sem.at[len(copies)])
                )
        fetch(copies)

    outs = [struct((2, count * span, share), BF16) for _ in range(replicas // 2)]
    scratch = [vmem(count, PIECES, r, h), vmem(replicas, count * span, share), sems(max(count, replicas))]
    return st.call(kernel, [st.where] + list(sources), outs, scratch, heavy=False, limit=12)


def stage_merge(st, parts, side=None):
    shape = parts[0].shape if side is None else parts[0].shape[1:]
    count = len(parts)

    def kernel(*refs):
        srcs, (out, buf, sem) = refs[:count], refs[count:]
        srcs = srcs if side is None else [one.at[side] for one in srcs]
        fetch([pltpu.make_async_copy(one, buf.at[i], sem.at[i]) for i, one in enumerate(srcs)])
        fetch([pltpu.make_async_copy(buf, out, sem.at[0])])

    outs = [struct((count,) + tuple(shape), BF16)]
    scratch = [vmem(count, *shape), sems(count)]
    return st.call(kernel, list(parts), outs, scratch, heavy=False)[0]


def stage_select(st, tail, kept, piece):
    r, w = st.rows, st.width

    def kernel(where, tail_r, kept_r, out, b, sem):
        @pl.when(where[0] == 0)
        def _():
            fetch([pltpu.make_async_copy(tail_r, b, sem.at[0])])

        @pl.when(where[0] != 0)
        def _():
            fetch([pltpu.make_async_copy(kept_r.at[piece], b, sem.at[0])])

        fetch([pltpu.make_async_copy(b, out, sem.at[0])])

    outs = [struct((r, w), BF16)]
    return st.call(kernel, [st.where, tail, kept], outs, [vmem(r, w), sems(1)], heavy=False)[0]


def stage_turn(st, near, far):
    share = far.shape[2]
    r = st.rows
    count = len(near)
    span = PIECES * r

    def kernel(*refs):
        near_r, refs = refs[:count], refs[count:]
        far_r, outs, (lb, ub, sem) = refs[0], refs[1 : 2 + PIECES], refs[2 + PIECES :]

        def gather(at, size, buf):
            rows = pl.ds(at, size)
            copies = []
            for q, one in enumerate(near_r):
                copies.append(pltpu.make_async_copy(one.at[0, rows, :], buf.at[pl.ds(q * size, size), :], sem.at[q]))
            for q in range(count):
                place = pl.ds((count + q) * size, size)
                copies.append(pltpu.make_async_copy(far_r.at[q, rows, :], buf.at[place, :], sem.at[count + q]))
            fetch(copies)

        for k in range(PIECES):
            gather(k * r, r, lb)
            outs[k][...] = lb[...].T
        gather(span, span, ub)
        outs[PIECES][...] = ub[...].T

    outs = [struct((share, 2 * count * r), BF16) for _ in range(PIECES)] + [struct((share, 2 * count * span), BF16)]
    vm, anyspace = pl.BlockSpec(memory_space=pltpu.VMEM), pl.BlockSpec(memory_space=pl.ANY)

    def wrapped(*refs):
        kernel(*refs[: count + 1], *refs[count + 2 :])

    call = pl.pallas_call(
        wrapped,
        out_shape=outs,
        in_specs=[anyspace] * (count + 2),
        out_specs=[vm] * len(outs),
        scratch_shapes=[vmem(2 * count * r, share), vmem(2 * count * span, share), sems(2 * count)],
        compiler_params=pltpu.CompilerParams(vmem_limit_bytes=16 * 2**20),
    )
    result = call(*near, far, st.token)
    st.token = result[0]
    return result[:PIECES], result[PIECES]


def stage_product(st, left, rights, before, members, lanes, gram):
    share, tokens = left.shape
    w = st.width
    step = tokens // len(rights)
    vm, anyspace = pl.BlockSpec(memory_space=pltpu.VMEM), pl.BlockSpec(memory_space=pl.ANY)
    extra = ([before] if before is not None else []) + ([gram] + list(members) if members else [])

    def kernel(left_r, *refs):
        right_r, refs = refs[: len(rights)], refs[len(rights) :]
        extra_r, refs = refs[: len(extra)], refs[len(extra) + 1 :]
        if members:
            out, sums, rb, rsem, tall = refs
        else:
            out, rb, rsem = refs
        fetch(
            [
                pltpu.make_async_copy(one, rb.at[pl.ds(p * step, step), :], rsem.at[p])
                for p, one in enumerate(right_r)
            ]
        )
        value = dot_nn(left_r[...], rb[...])
        if before is not None:
            value = value + extra_r[0][...]
        out[...] = value
        if members:
            gram_r, older, prev, cur = extra_r[1:]
            size = row_block(share)
            tall[...] = jnp.zeros_like(tall)

            def run(i, carry):
                block = pl.ds(pl.multiple_of(i * size, size), size)
                mine = out[block, :]
                others = [older[j, block, :] for j in range(older.shape[0])] + [prev[block, :], cur[block, :], mine]
                for j, other in enumerate(others):
                    tall[j : j + 1, :] += jnp.sum(mine * other, axis=0, keepdims=True)
                return carry

            lax.fori_loop(0, share // size, run, 0)
            total = gram_r[...]
            for j, lane in enumerate(lanes):
                total = total + jnp.where(lane_of(lane), jnp.sum(tall[j : j + 1, :]), 0.0)
            sums[...] = total

    outs = [struct((share, w), F32)] + ([struct((1, 128), F32)] if members else [])
    call = pl.pallas_call(
        kernel,
        out_shape=outs,
        in_specs=[vm] + [anyspace] * len(rights) + [vm] * len(extra) + [anyspace],
        out_specs=[vm] * len(outs),
        scratch_shapes=[vmem(tokens, w), sems(len(rights))] + ([vmem(8, w, dtype=F32)] if members else []),
        compiler_params=pltpu.CompilerParams(vmem_limit_bytes=32 * 2**20),
    )
    result = call(left, *rights, *extra, st.token)
    st.token = result[0]
    return result


def stage_cross(st, pairs, feed, theirs):
    r, w = st.rows, st.width
    half = st.dirs.shape[0]

    def kernel(where, feed_r, theirs_r, dirs, back, mine, fb, mb, bb, sem):
        live, _ = pick(where[0], pairs)

        @pl.when(live)
        def _():
            fetch(
                [
                    pltpu.make_async_copy(theirs_r, fb.at[pl.ds(0, r), :], sem.at[0]),
                    pltpu.make_async_copy(feed_r, fb.at[pl.ds(r, r), :], sem.at[1]),
                ]
            )
            both = dot_nt(fb[...], dirs[...])
            bb[...] = both[:r].astype(BF16)
            mb[...] = both[r:]
            fetch([pltpu.make_async_copy(bb, back, sem.at[0]), pltpu.make_async_copy(mb, mine, sem.at[1])])

    outs = [struct((r, half), BF16), struct((r, half), F32)]
    scratch = [vmem(2 * r, w), vmem(r, half, dtype=F32), vmem(r, half), sems(2)]
    return st.call(kernel, [st.where, feed, theirs, st.dirs], outs, scratch, heavy=False)


def stage_curve(st, pairs, last, row_count, arrived, top, v_recv, v_mine, forward, tang, grads, state):
    r, w, h = st.rows, st.width, st.hidden
    held = 1 if state else 0
    half = h // 2

    def kernel(*refs):
        where, arr, top_r, vr, vm, gain, win, wout, x_st, pre_st, tan_st, pd_st, back_r, ng_r = refs[:14]
        send, gd_st, acc, sem = refs[14 + held : 18 + held]
        gb, xb, tb, preb, pdb, backb, vb, vrb, vmb, ngb, sendb = refs[18 + held :]
        section, upper = where[0], where[1]
        live, k = pick(section, pairs)

        @pl.when(live)
        def _():
            takes = [
                pltpu.make_async_copy(x_st.at[k], xb, sem.at[1]),
                pltpu.make_async_copy(tan_st.at[k], tb, sem.at[2]),
                pltpu.make_async_copy(pre_st.at[k], preb, sem.at[3]),
                pltpu.make_async_copy(pd_st.at[k], pdb, sem.at[4]),
                pltpu.make_async_copy(back_r, backb, sem.at[5]),
                pltpu.make_async_copy(vr, vrb, sem.at[6]),
                pltpu.make_async_copy(vm, vmb, sem.at[7]),
                pltpu.make_async_copy(ng_r, ngb, sem.at[8]),
            ]
            grad_in = pltpu.make_async_copy(arr, gb, sem.at[0])
            top_in = pltpu.make_async_copy(top_r, gb, sem.at[0])

            @pl.when(section == last)
            def _():
                top_in.start()

            @pl.when(section != last)
            def _():
                grad_in.start()

            for one in takes:
                one.start()
            grad_in.wait()

            @pl.when(section == last)
            def _():
                gb[...] = (gb[...].astype(F32) / row_count).astype(BF16)

            for one in takes:
                one.wait()

            @pl.when(upper == 0)
            def _():
                vb[:, :half] = vmb[...]
                vb[:, half:] = vrb[...].astype(F32)

            @pl.when(upper != 0)
            def _():
                vb[:, :half] = vrb[...].astype(F32)
                vb[:, half:] = vmb[...]

            grad_dot = gb[...]
            acc[...] = jnp.zeros_like(acc)

            def step(j, cols):
                back_dot = dot_nn(grad_dot, wout[:, cols]) + vb[:, cols]
                slope, bend = gelu_slope_bend(preb[:, cols])
                pre_grad_dot = bend * pdb[:, cols] * backb[:, cols] + slope * back_dot
                acc[...] += dot_nt(pre_grad_dot.astype(BF16), win[:, cols])

            st.sweep(step)
            tan = tb[...].astype(F32)
            x_hat, scale = standardize(xb[...].astype(F32))
            shift = tan - mean_of(tan)
            slant = mean_of(x_hat * shift)
            hat_dot = scale * (shift - x_hat * slant)
            scale_dot = -scale * scale * slant
            h_grad = ngb[...] * gain[...]
            h_dot = acc[...] * gain[...]
            along = mean_of(h_grad * x_hat)
            pull = h_grad - mean_of(h_grad) - x_hat * along
            along_dot = mean_of(h_dot * x_hat + h_grad * hat_dot)
            pull_dot = h_dot - mean_of(h_dot) - hat_dot * along - x_hat * along_dot
            move = scale_dot * pull + scale * pull_dot
            sendb[...] = (grad_dot.astype(F32) + move).astype(BF16)
            fetch(
                [
                    pltpu.make_async_copy(sendb, send, sem.at[9]),
                    pltpu.make_async_copy(gb, gd_st.at[k], sem.at[10]),
                ]
            )

    outs = [struct((r, w), BF16), struct((PIECES, r, w), BF16)]
    scratch = st.accumulator() + [
        sems(11), vmem(r, w), vmem(r, w), vmem(r, w), vmem(r, h, dtype=F32), vmem(r, h, dtype=F32),
        vmem(r, h, dtype=F32), vmem(r, h, dtype=F32), vmem(r, half), vmem(r, half, dtype=F32),
        vmem(r, w, dtype=F32), vmem(r, w),
    ]
    arrays = [st.where, arrived, top, v_recv, v_mine, st.gain, st.w_in, st.w_out_t]
    arrays += [forward[1], forward[2], tang[1], tang[2], grads[3], grads[4]]
    arrays += state[1:2] if state else []
    return st.call(kernel, arrays, outs, scratch, {14: 1} if state else {})


def row_block(rows):
    for size in range(min(rows, 80), 0, -1):
        if rows % size == 0 and size % 8 == 0:
            return size
    return rows


def lane_of(at):
    return lax.broadcasted_iota(jnp.int32, (1, 128), 1) == at


def inner_products(st, older, prev, cur, lanes):
    rows = cur.shape[0]
    size = row_block(rows)

    def kernel(older_r, prev_r, cur_r, token, out, tall):
        tall[...] = jnp.zeros_like(tall)

        def run(i, carry):
            block = pl.ds(pl.multiple_of(i * size, size), size)
            values = [older_r[j, block, :] for j in range(older_r.shape[0])] + [prev_r[block, :], cur_r[block, :]]
            for j, (a, b) in enumerate(lanes):
                tall[j : j + 1, :] += jnp.sum(values[a] * values[b], axis=0, keepdims=True)
            return carry

        lax.fori_loop(0, rows // size, run, 0)
        total = jnp.zeros((1, 128), F32)
        for j, lane in enumerate(lanes.values()):
            total = total + jnp.where(lane_of(lane), jnp.sum(tall[j : j + 1, :]), 0.0)
        out[...] = total

    vm = pl.BlockSpec(memory_space=pltpu.VMEM)
    call = pl.pallas_call(
        kernel,
        out_shape=struct((1, 128), F32),
        in_specs=[vm] * 3 + [pl.BlockSpec(memory_space=pl.ANY)],
        out_specs=vm,
        scratch_shapes=[vmem(-(-len(lanes) // 8) * 8, cur.shape[1], dtype=F32)],
        compiler_params=pltpu.CompilerParams(vmem_limit_bytes=20 * 2**20),
    )
    st.token = call(older, prev, cur, st.token)
    return st.token


def finish(packed, beta_old, hvp, members, gram_at, cross_at, square_at, entry_count):
    rows, width = hvp.shape
    count = members[0].shape[0] + 2
    size = row_block(rows)

    def kernel(packed_r, beta_r, hvp_r, older, before, now, out, entries):
        mean = lambda lane: packed_r[0, lane] / entry_count
        gram = {key: mean(lane) for key, lane in gram_at.items()}
        cross = [mean(lane) for lane in cross_at]
        square = mean(square_at)
        g = lambda i, j: gram[min(i, j), max(i, j)]
        prev, cur = count - 2, count - 1
        old = beta_r[0]
        alpha = cross[cur] - old * g(prev, cur)
        weights = [cross[j] - old * g(prev, j) - alpha * g(cur, j) for j in range(count)]
        weights[prev] = weights[prev] + old
        weights[cur] = weights[cur] + alpha
        norm = square
        for i in range(count):
            inner = 2.0 * cross[i]
            for j in range(count):
                inner = inner - weights[j] * g(i, j)
            norm = norm - weights[i] * inner
        beta = jnp.sqrt(jnp.full((1, 128), jnp.maximum(norm, 0.0) + 1e-06, F32))
        entries[...] = jnp.where(lane_of(0), alpha, beta)
        wide = beta[:, :1]

        def run(i, carry):
            block = pl.ds(pl.multiple_of(i * size, size), size)
            value = hvp_r[block, :]
            parts = [older[j, block, :] for j in range(count - 2)] + [before[block, :], now[block, :]]
            for weight, part in zip(weights, parts):
                value = value - weight * part
            out[block, :] = value / wide
            return carry

        lax.fori_loop(0, rows // size, run, 0)

    vm = pl.BlockSpec(memory_space=pltpu.VMEM)
    sm = pl.BlockSpec(memory_space=pltpu.SMEM)
    return pl.pallas_call(
        kernel,
        out_shape=[struct((rows, width), F32), struct((1, 128), F32)],
        in_specs=[sm, sm] + [vm] * 4,
        out_specs=[vm, vm],
        compiler_params=pltpu.CompilerParams(vmem_limit_bytes=48 * 2**20),
        name="finish",
    )(packed, beta_old, hvp, *members)


def shift(value, pairs, step):
    return lax.ppermute(value, "section", [(s, s + step) for s, _ in pairs])


def tick_pairs(tick, sections, start, up):
    found = []
    for s in range(sections):
        k = tick - (s if up else sections - 1 - s)
        if 0 <= k < PIECES and s >= start:
            found.append((s, k))
    return found


def gather_pieces(block, replicas):
    found = {0: block}
    bits = [1 << i for i in range(1, replicas.bit_length() - 2)] + [1]
    for bit in bits:
        for offset in list(found):
            found[offset | bit] = lax.ppermute(found[offset], "dp", xor_pairs(replicas, bit))
    return found


def send_column(block, replicas):
    found = [block]
    for offset in range(2, replicas, 2):
        found.append(lax.ppermute(block, "dp", xor_pairs(replicas, offset)))
    return found


def trade_column(blocks, replicas):
    found = [blocks[0]]
    for q in range(1, replicas // 2):
        found.append(lax.ppermute(blocks[q], "dp", xor_pairs(replicas, 2 * q)))
    return found


def swap(block, replicas):
    return lax.ppermute(block, "dp", xor_pairs(replicas, 1))


def reduce_all(value, sections, replicas):
    for axis, count in (("dp", replicas), ("section", sections)):
        bit = 1
        while bit < count:
            value = value + lax.ppermute(value, axis, xor_pairs(count, bit))
            bit *= 2
    return value


def body(
    inputs,
    targets,
    weight_in,
    hidden_bias,
    norm_gain,
    weight_out,
    current,
    previous,
    older_basis,
    beta_before,
):
    section = lax.axis_index("section")
    replica = lax.axis_index("dp")
    sections = lax.axis_size("section")
    replicas = lax.axis_size("dp")
    last = sections - 1
    top_bit = replicas // 2
    local_rows, width = inputs.shape
    hidden = weight_in.shape[2]
    rows = local_rows // PIECES
    share = hidden // replicas
    row_count = float(local_rows * replicas)
    upper = (replica & top_bit) != 0
    numbers = [section, upper, replica, replica & (top_bit - 1)]
    where = jnp.stack([one.astype(jnp.int32) for one in numbers])
    st = Stage(rows, width, hidden, where, weight_in[0], weight_out[0].T, norm_gain)
    feed = inputs.reshape(PIECES, rows, width)
    goal = targets.reshape(PIECES, rows, width)
    partner = xor_pairs(replicas, top_bit)
    both_axes = ("section", "dp")

    def cross_pairs(pairs):
        return [
            (s * replicas + i, s * replicas + (i ^ top_bit)) for s, _ in pairs for i in range(replicas)
        ]

    own_direction = current[0].astype(BF16)
    pieces = gather_pieces(own_direction, replicas)
    if share % 16:
        held = jnp.stack([pieces[offset] for offset in sorted(pieces)])
        order = (replica & (top_bit - 1)) ^ jnp.arange(top_bit)
        pieces = {0: held[order].reshape(-1, width)}

    forward, arrived = None, feed[0]
    tops = {}
    for tick in range(sections + PIECES - 1):
        pairs = tick_pairs(tick, sections, 0, True)
        forward = stage_forward(st, pairs, feed, arrived, hidden_bias, forward, (goal, own_direction))
        if tick >= last:
            tops[tick - last] = forward[0]
        going = [(s, k) for s, k in pairs if s < last]
        if going:
            arrived = shift(forward[0], going, 1)
    hid_st = forward[3]

    hid_theirs = lax.ppermute(forward[5], "dp", partner)

    grads, g_arr = None, feed[0]
    crossed = []

    def run_gradient(tick):
        nonlocal grads, g_arr
        pairs = tick_pairs(tick, sections, 1, False)
        top = tops.get(tick, g_arr)
        grads = stage_gradient(st, pairs, last, row_count, g_arr, top, goal, forward, grads)
        going = [(s, k) for s, k in pairs if s > 1]
        if going:
            g_arr = shift(grads[0], going, -1)
        theirs = lax.ppermute(grads[2], both_axes, cross_pairs(pairs))
        crossed.append((pairs, grads, theirs))

    v_terms = {}

    def run_cross(tick):
        pairs, held, theirs = crossed[tick]
        back, mine = stage_cross(st, pairs, held[2], theirs)
        came = lax.ppermute(back, both_axes, cross_pairs(pairs))
        v_terms[tick] = (came, mine)

    run_gradient(0)
    u_theirs, u_mine = stage_direction(st, pieces, hid_theirs, forward[4])
    u_recv = []
    for i in range(PIECES):
        u_recv.append(lax.ppermute(u_theirs[i], "dp", partner))
    from_first = []

    def run_first(i):
        from_first.append(shift(stage_first(st, u_mine, u_recv[i], i), [(0, 0)], 1))

    tang, t_arr = None, feed[0]
    t_tops = {}

    def run_tangent(tick):
        nonlocal tang, t_arr
        pairs = tick_pairs(tick, sections, 1, True)
        came = from_first[min(tick - 1, PIECES - 1)]
        held = [u_recv[max(k for _, k in pairs) if i else 0] for i in range(2)]
        tang = stage_tangent(st, pairs, came, t_arr, u_mine, held, forward, tang)
        if tick >= last:
            t_tops[tick - last] = tang[0]
        going = [(s, k) for s, k in pairs if s < last]
        if going:
            t_arr = shift(tang[0], going, 1)

    curve, d_arr = None, feed[0]
    tail = {}

    def run_curve(tick):
        nonlocal curve, d_arr
        pairs = tick_pairs(tick, sections, 1, False)
        top = t_tops.get(tick, d_arr)
        v_recv, v_mine = v_terms[tick]
        curve = stage_curve(
            st, pairs, last, row_count, d_arr, top, v_recv, v_mine, forward, tang,
            crossed[tick][1], curve,
        )
        d_arr = shift(curve[0], pairs, -1)
        for s, k in pairs:
            if s == 1:
                tail[k] = d_arr

    older = older_basis[:, 0]
    members = [older, previous[0], current[0]]
    count = older.shape[0] + 2
    keys = [(i, j) for i in range(count) for j in range(i, count)]
    gram_at = {key: lane for lane, key in enumerate(keys)}
    cross_at = [len(keys) + i for i in range(count)]
    square_at = len(keys) + count

    run_gradient(1)
    run_first(0)
    run_cross(0)
    run_tangent(1)
    run_first(1)
    run_tangent(2)
    run_cross(1)
    run_tangent(3)
    run_gradient(2)
    run_curve(0)
    run_tangent(4)
    blocks = trade_column(stage_split(st, [hid_st, tang[3]], replicas), replicas)
    run_curve(1)
    run_cross(2)
    run_gradient(3)
    run_cross(3)
    grad_column = send_column(grads[1], replicas)
    run_curve(2)
    columns = []

    def run_tail(i):
        block = stage_select(st, tail[i], curve[1], i)
        columns.append(send_column(block, replicas))

    gram = inner_products(st, *members, gram_at)
    run_tail(0)
    run_curve(3)
    far = swap(stage_merge(st, blocks, 1), replicas)
    run_tail(1)
    grad_near = stage_merge(st, grad_column)
    grad_far = swap(grad_near, replicas)
    hid_turned, slope_turned = stage_turn(st, blocks, far)
    nears = [stage_merge(st, columns[0])]
    fars = [swap(nears[0], replicas)]
    flat = lambda one: one.reshape(-1, width)
    total = stage_product(st, slope_turned, [flat(grad_near), flat(grad_far)], None, None, None, None)[0]
    for k in range(PIECES):
        if k > 0:
            nears.append(stage_merge(st, columns[k]))
            fars.append(swap(nears[k], replicas))
        ending = (members, cross_at + [square_at], gram) if k == PIECES - 1 else (None, None, None)
        product = stage_product(st, hid_turned[k], [flat(nears[k]), flat(fars[k])], total, *ending)
        total = product[0]
    hvp, local = product

    entry_count = float(share * width * sections * replicas)
    packed = reduce_all(local, sections, replicas)
    vector, entries = finish(
        packed, beta_before, hvp, members, gram_at, cross_at, square_at, entry_count
    )
    return (vector[None], entries[0, :2])


def solution(mesh):
    return jax.shard_map(
        body,
        mesh=mesh,
        in_specs=(
            P("dp", None),
            P("dp", None),
            P("section", None, None),
            P("section", None),
            P("section", None),
            P("section", None, None),
            P("section", "dp", None),
            P("section", "dp", None),
            P(None, "section", "dp", None),
            P(),
        ),
        out_specs=(P("section", "dp", None), P()),
        check_vma=False,
    )
```

```python
import math

import jax
import jax.numpy as jnp
from jax import lax
from jax.experimental import pallas as pl
from jax.experimental.pallas import tpu as pltpu
from jax.sharding import PartitionSpec as P

F32 = jnp.float32
BF16 = jnp.bfloat16
PIECES = 2
UNROLL = False
ROOT = 0.7978845608028654
CUBE = 0.044715
EPS = 1e-05


def chunk_of(width):
    for parts in range(1, width + 1):
        if width % parts == 0 and width // parts <= 640 and (width // parts) % 128 == 0:
            return width // parts
    return width


def gelu_parts(v):
    square = v * v
    t = jnp.tanh(ROOT * v * (1.0 + CUBE * square))
    return square, t


def gelu_value(v):
    _, t = gelu_parts(v)
    return 0.5 * v * (1.0 + t)


def gelu_slope(v):
    square, t = gelu_parts(v)
    rise = ROOT * (1.0 + 3.0 * CUBE * square)
    return 0.5 * (1.0 + t) + 0.5 * v * (1.0 - t * t) * rise


def gelu_slope_bend(v):
    square, t = gelu_parts(v)
    rise = ROOT * (1.0 + 3.0 * CUBE * square)
    fall = 1.0 - t * t
    slope = 0.5 * (1.0 + t) + 0.5 * v * fall * rise
    bend = fall * (rise + v * (3.0 * ROOT * CUBE * v - t * rise * rise))
    return slope, bend


def mean_of(v):
    return jnp.mean(v, axis=-1, keepdims=True)


def standardize(x):
    centered = x - mean_of(x)
    scale = lax.rsqrt(mean_of(centered * centered) + EPS)
    return centered * scale, scale


def dot_nn(a, b):
    return lax.dot_general(a, b, (((1,), (0,)), ((), ())), preferred_element_type=F32)


def dot_nt(a, b):
    return lax.dot_general(a, b, (((1,), (1,)), ((), ())), preferred_element_type=F32)


def xor_pairs(count, bit):
    return [(i, i ^ bit) for i in range(count)]


class Stage:
    def __init__(self, rows, width, hidden, where, w_in, w_out_t, gain):
        self.rows, self.width, self.hidden = rows, width, hidden
        self.chunk = chunk_of(hidden)
        self.parts = hidden // self.chunk
        self.where, self.w_in, self.w_out_t, self.gain = where, w_in, w_out_t, gain
        self.token = gain
        self.dirs = None

    def accumulator(self):
        return [pltpu.VMEM((self.rows, self.width), F32)]

    def sweep(self, step):
        if UNROLL:
            for j in range(self.parts):
                step(j, slice(j * self.chunk, (j + 1) * self.chunk))
            return

        def run(j, carry):
            step(j, pl.ds(pl.multiple_of(j * self.chunk, self.chunk), self.chunk))
            return carry

        lax.fori_loop(0, self.parts, run, 0)

    def call(self, kernel, arrays, outs, scratch, aliases=None, heavy=True, load=False, kept=(), limit=8):
        count = len(arrays)
        spec = []
        for one in arrays:
            if one is self.dirs:
                spec.append(pl.BlockSpec(memory_space=pltpu.VMEM))
            elif one is self.w_in or one is self.w_out_t:
                spec.append(pl.BlockSpec(memory_space=pl.ANY if load else pltpu.VMEM))
            elif one.dtype == jnp.int32:
                spec.append(pl.BlockSpec(memory_space=pltpu.SMEM))
            elif one.ndim == 2 and one.shape[0] == 1:
                spec.append(pl.BlockSpec(memory_space=pltpu.VMEM))
            else:
                spec.append(pl.BlockSpec(memory_space=pl.ANY))

        def wrapped(*refs):
            kernel(*refs[:count], *refs[count + 1 :])

        kept = [pltpu.VMEM(shape, dtype) for shape, dtype in kept]
        out_spec = [pl.BlockSpec(memory_space=pl.ANY) for _ in outs]
        out_spec += [pl.BlockSpec(memory_space=pltpu.VMEM) for _ in kept]
        result = pl.pallas_call(
            wrapped,
            out_shape=outs + kept,
            in_specs=spec + [pl.BlockSpec(memory_space=pl.ANY)],
            out_specs=out_spec,
            scratch_shapes=scratch,
            input_output_aliases=aliases or {},
            compiler_params=pltpu.CompilerParams(vmem_limit_bytes=limit * 2**20),
            cost_estimate=pl.CostEstimate(
                flops=4 * self.rows * self.width * self.hidden if heavy else 1000,
                bytes_accessed=4 * self.width * self.hidden if heavy else 1000,
                transcendentals=0,
            ),
        )
        result = list(result(*arrays, self.token))
        self.token = result[0]
        return result


def fetch(copies):
    for one in copies:
        one.start()
    for one in copies:
        one.wait()


def choose(section, options, buf, sem):
    copies = [(s, pltpu.make_async_copy(one, buf, sem)) for s, one in options]
    hit = False
    for s, one in copies:
        hit = jnp.logical_or(hit, section == s)

        @pl.when(section == s)
        def _(one=one):
            one.start()

    def wait():
        @pl.when(hit)
        def _():
            copies[0][1].wait()

    return wait


def struct(shape, dtype):
    return jax.ShapeDtypeStruct(shape, dtype)


def vmem(*shape, dtype=BF16):
    return pltpu.VMEM(shape, dtype)


def sems(count):
    return pltpu.SemaphoreType.DMA((count,))


def pick(section, pairs):
    live, piece = False, 0
    for s, k in pairs:
        hit = section == s
        live = jnp.logical_or(live, hit)
        piece = piece + jnp.where(hit, k, 0)
    return live, piece


def stage_forward(st, pairs, inputs, arrived, bias, load, extra=()):
    r, w, h = st.rows, st.width, st.hidden
    held = len(extra)

    def kernel(*refs):
        where, inp, arr, bias_r, gain, win, wout = refs[:7]
        send, x_o, pre_o, hid_o = refs[7 + held : 11 + held]
        rest = refs[11 + held :]
        if load:
            win_v, wout_v, rest = rest[0], rest[1], rest[2:]
        acc, sem, xb, preb, hidb, sendb = rest[:6]
        section = where[0]
        live, k = pick(section, pairs)
        if load:
            wsem = rest[6]

            def flow(row, j):
                cols = pl.ds(pl.multiple_of(j * st.chunk, st.chunk), st.chunk)
                source, target = ((win, win_v), (wout, wout_v))[row]
                return pltpu.make_async_copy(source.at[:, cols], target.at[:, cols], wsem.at[row, j])

            for j in range(st.parts):
                flow(0, j).start()
                flow(1, j).start()

            @pl.when(jnp.logical_not(live))
            def _():
                for j in range(st.parts):
                    flow(0, j).wait()
                    flow(1, j).wait()

        in_w, out_w = (win_v, wout_v) if load else (win, wout)

        @pl.when(live)
        def _():
            own = pltpu.make_async_copy(inp.at[k], xb, sem.at[0])
            other = pltpu.make_async_copy(arr, xb, sem.at[0])

            @pl.when(section == 0)
            def _():
                own.start()

            @pl.when(section != 0)
            def _():
                other.start()

            other.wait()
            x = xb[...].astype(F32)
            x_hat, _ = standardize(x)
            normed = (x_hat * gain[...]).astype(BF16)
            acc[...] = x

            def step(j, cols):
                if load:
                    flow(0, j).wait()
                pre = dot_nn(normed, in_w[:, cols]) + bias_r[:, cols]
                preb[:, cols] = pre
                hid = gelu_value(pre).astype(BF16)
                hidb[:, cols] = hid
                if load:
                    flow(1, j).wait()
                acc[...] += dot_nt(hid, out_w[:, cols])

            st.sweep(step)
            sendb[...] = acc[...].astype(BF16)
            fetch(
                [
                    pltpu.make_async_copy(sendb, send, sem.at[1]),
                    pltpu.make_async_copy(xb, x_o, sem.at[2]),
                    pltpu.make_async_copy(preb, pre_o, sem.at[3]),
                    pltpu.make_async_copy(hidb, hid_o, sem.at[4]),
                ]
            )

    outs = [struct((r, w), BF16), struct((r, w), BF16), struct((r, h), F32), struct((r, h), BF16)]
    scratch = st.accumulator() + [sems(5), vmem(r, w), vmem(r, h, dtype=F32), vmem(r, h), vmem(r, w)]
    arrays = [st.where, inputs, arrived, bias, st.gain, st.w_in, st.w_out_t]
    if not load:
        return st.call(kernel, arrays, outs, scratch)
    scratch.append(pltpu.SemaphoreType.DMA((2, st.parts)))
    kept = [((w, h), BF16)] * 2
    result = st.call(kernel, arrays + list(extra), outs, scratch, load=True, kept=kept, limit=36)
    st.w_in, st.w_out_t = result[-2:]
    return result[:-2]


def stage_tangent(st, pairs, from_first, arrived, u_mine, u_recv, forward):
    r, w, h = st.rows, st.width, st.hidden

    def kernel(*refs):
        where, arr0, arr, um, ur0, ur1, gain, win, wout, x_st, pre_st = refs[:11]
        send, tan_o, pd_o, hd_o, acc, sem = refs[11:17]
        tb, xb, preb, pdb, hdb, umb, urb, sendb = refs[17:]
        section = where[0]
        live, k = pick(section, pairs)

        @pl.when(live)
        def _():
            came0 = pltpu.make_async_copy(arr0, tb, sem.at[2])
            came = pltpu.make_async_copy(arr, tb, sem.at[2])
            back0 = pltpu.make_async_copy(ur0, urb, sem.at[1])
            back1 = pltpu.make_async_copy(ur1, urb, sem.at[1])
            mine = pltpu.make_async_copy(um.at[k], umb, sem.at[0])
            takes = [
                pltpu.make_async_copy(x_st, xb, sem.at[3]),
                pltpu.make_async_copy(pre_st, preb, sem.at[4]),
            ]

            @pl.when(section == 1)
            def _():
                came0.start()

            @pl.when(section != 1)
            def _():
                came.start()

            for one in takes:
                one.start()
            mine.start()

            @pl.when(k == 0)
            def _():
                back0.start()

            @pl.when(k != 0)
            def _():
                back1.start()

            came.wait()
            for one in takes:
                one.wait()
            tan = tb[...].astype(F32)
            x_hat, scale = standardize(xb[...].astype(F32))
            shift = tan - mean_of(tan)
            normed_dot = (gain[...] * scale * (shift - x_hat * mean_of(x_hat * shift))).astype(BF16)
            acc[...] = tan

            def step(j, cols):
                pre_dot = dot_nn(normed_dot, win[:, cols])
                pdb[:, cols] = pre_dot
                hid_dot = (gelu_slope(preb[:, cols]) * pre_dot).astype(BF16)
                hdb[:, cols] = hid_dot
                acc[...] += dot_nt(hid_dot, wout[:, cols])

            st.sweep(step)
            mine.wait()
            back0.wait()
            sendb[...] = (acc[...] + umb[...] + urb[...].astype(F32)).astype(BF16)
            fetch(
                [
                    pltpu.make_async_copy(sendb, send, sem.at[5]),
                    pltpu.make_async_copy(tb, tan_o, sem.at[6]),
                    pltpu.make_async_copy(pdb, pd_o, sem.at[7]),
                    pltpu.make_async_copy(hdb, hd_o, sem.at[8]),
                ]
            )

    outs = [
        struct((r, w), BF16),
        struct((r, w), BF16),
        struct((r, h), F32),
        struct((r, h), BF16),
    ]
    scratch = st.accumulator() + [
        sems(9), vmem(r, w), vmem(r, w), vmem(r, h, dtype=F32), vmem(r, h, dtype=F32), vmem(r, h),
        vmem(r, w, dtype=F32), vmem(r, w), vmem(r, w),
    ]
    arrays = [st.where, from_first, arrived, u_mine, u_recv[0], u_recv[1], st.gain, st.w_in, st.w_out_t]
    arrays += [forward[1], forward[2]]
    return st.call(kernel, arrays, outs, scratch)


def stage_gradient(st, pairs, last, row_count, arrived, top, goal, forwards):
    r, w, h = st.rows, st.width, st.hidden
    count = len(pairs)

    def kernel(*refs):
        where, arr, top_r, goal_r, gain, win, wout = refs[:7]
        x_rs, pre_rs, refs = refs[7 : 7 + count], refs[7 + count : 7 + 2 * count], refs[7 + 2 * count :]
        send, feed, back_o, ng_o, acc, sem = refs[:6]
        gb, tb, xb, preb, backb, sendb = refs[6:]
        section = where[0]
        live, k = pick(section, pairs)

        @pl.when(live)
        def _():
            sites = [s for s, _ in pairs]
            waits = [
                choose(section, list(zip(sites, x_rs)), xb, sem.at[2]),
                choose(section, list(zip(sites, pre_rs)), preb, sem.at[3]),
            ]
            grad_in = pltpu.make_async_copy(arr, gb, sem.at[0])
            top_in = pltpu.make_async_copy(top_r, gb, sem.at[0])
            goal_in = pltpu.make_async_copy(goal_r.at[k], tb, sem.at[1])

            @pl.when(section == last)
            def _():
                top_in.start()
                goal_in.start()

            @pl.when(section != last)
            def _():
                grad_in.start()

            grad_in.wait()

            @pl.when(section == last)
            def _():
                goal_in.wait()
                gap = gb[...].astype(F32) - tb[...].astype(F32)
                gb[...] = (gap / row_count).astype(BF16)

            for wait in waits:
                wait()
            grad = gb[...]
            x_hat, scale = standardize(xb[...].astype(F32))
            acc[...] = jnp.zeros_like(acc)

            def step(j, cols):
                back = dot_nn(grad, wout[:, cols])
                backb[:, cols] = back
                pre_grad = (gelu_slope(preb[:, cols]) * back).astype(BF16)
                acc[...] += dot_nt(pre_grad, win[:, cols])

            st.sweep(step)
            h_grad = acc[...] * gain[...]
            move = scale * (h_grad - mean_of(h_grad) - x_hat * mean_of(h_grad * x_hat))
            sendb[...] = (grad.astype(F32) + move).astype(BF16)
            fetch(
                [
                    pltpu.make_async_copy(sendb, send, sem.at[4]),
                    pltpu.make_async_copy(backb, back_o, sem.at[6]),
                    pltpu.make_async_copy(acc, ng_o, sem.at[7]),
                    pltpu.make_async_copy(gb, feed, sem.at[8]),
                ]
            )

    outs = [
        struct((r, w), BF16),
        struct((r, w), BF16),
        struct((r, h), F32),
        struct((r, w), F32),
    ]
    scratch = st.accumulator() + [
        sems(9), vmem(r, w), vmem(r, w), vmem(r, w), vmem(r, h, dtype=F32), vmem(r, h, dtype=F32), vmem(r, w),
    ]
    arrays = [st.where, arrived, top, goal, st.gain, st.w_in, st.w_out_t]
    arrays += [one[1] for one in forwards] + [one[2] for one in forwards]
    return st.call(kernel, arrays, outs, scratch)


def stage_direction(st, pieces, theirs, mine):
    r, w = st.rows, st.width
    offsets = sorted(pieces)
    half = mine.shape[2]
    block = half // len(offsets)

    def kernel(where, theirs_r, mine_r, *refs):
        parts, refs = refs[: len(offsets)], refs[len(offsets) :]
        backs, u_mine, dirs, fb, ub, bb, sem, psem = refs[:PIECES], *refs[PIECES:]
        low = where[3]
        copies = []
        for i, offset in enumerate(offsets):
            place = 0
            if len(offsets) > 1:
                place = pl.multiple_of((low ^ offset) * block, math.gcd(block, 16))
            copies.append(pltpu.make_async_copy(parts[i], dirs.at[pl.ds(place, block), :], psem.at[i]))
        copies.append(pltpu.make_async_copy(theirs_r, fb.at[pl.ds(0, PIECES)], sem.at[0]))
        copies.append(pltpu.make_async_copy(mine_r, fb.at[pl.ds(PIECES, PIECES)], sem.at[1]))
        fetch(copies)
        both = dot_nn(fb[...].reshape(2 * PIECES * r, half), dirs[...])
        for i in range(PIECES):
            bb[i] = both[i * r : (i + 1) * r].astype(BF16)
            ub[i] = both[(PIECES + i) * r : (PIECES + i + 1) * r]
        copies = [pltpu.make_async_copy(bb.at[i], backs[i], psem.at[i]) for i in range(PIECES)]
        fetch(copies + [pltpu.make_async_copy(ub, u_mine, sem.at[0])])

    outs = [struct((r, w), BF16) for _ in range(PIECES)] + [struct((PIECES, r, w), F32)]
    scratch = [
        vmem(2 * PIECES, r, half),
        vmem(PIECES, r, w, dtype=F32),
        vmem(PIECES, r, w),
        sems(2),
        sems(max(PIECES, len(offsets))),
    ]
    arrays = [st.where, theirs, mine] + [pieces[offset] for offset in offsets]
    result = st.call(kernel, arrays, outs, scratch, heavy=False, kept=[((half, w), BF16)], limit=12)
    st.dirs = result[-1]
    return result[:PIECES], result[PIECES]


def stage_first(st, u_mine, u_recv, piece):
    r, w = st.rows, st.width

    def kernel(where, um, ur, send, a, b, c, sem):
        @pl.when(where[0] == 0)
        def _():
            fetch([pltpu.make_async_copy(um.at[piece], a, sem.at[0]), pltpu.make_async_copy(ur, b, sem.at[1])])
            c[...] = (a[...] + b[...].astype(F32)).astype(BF16)
            fetch([pltpu.make_async_copy(c, send, sem.at[0])])

    scratch = [vmem(r, w, dtype=F32), vmem(r, w), vmem(r, w), sems(2)]
    return st.call(kernel, [st.where, u_mine, u_recv], [struct((r, w), BF16)], scratch, heavy=False)[0]


def take_pieces(section, choices, buf, sem):
    waits = []
    for k, options in enumerate(choices):
        hit = False
        for s, _ in options:
            hit = jnp.logical_or(hit, section == s)

        @pl.when(jnp.logical_not(hit))
        def _(k=k):
            buf[k] = jnp.zeros(buf.shape[1:], buf.dtype)

        waits.append(choose(section, options, buf.at[k], sem.at[k]))
    for wait in waits:
        wait()


def listed(choices):
    arrays = []
    for options in choices:
        for _, one in options:
            if not any(one is other for other in arrays):
                arrays.append(one)
    return arrays


def placed(choices, arrays, refs):
    at = lambda one: [i for i, other in enumerate(arrays) if other is one][0]
    return [[(s, refs[at(one)]) for s, one in options] for options in choices]


def stage_halves(st, choices):
    r, h = st.rows, st.hidden
    half = h // 2
    arrays = listed(choices)

    def kernel(where, *refs):
        mine, theirs, sb, hb, sem = refs[len(arrays) :]
        take_pieces(where[0], placed(choices, arrays, refs), sb, sem)
        upper = where[1]
        for k in range(PIECES):
            hb[0, k] = sb[k, :, :half]
            hb[1, k] = sb[k, :, half:]
        fetch(
            [
                pltpu.make_async_copy(hb.at[upper], mine, sem.at[0]),
                pltpu.make_async_copy(hb.at[1 - upper], theirs, sem.at[1]),
            ]
        )

    outs = [struct((PIECES, r, half), BF16)] * 2
    scratch = [vmem(PIECES, r, h), vmem(2, PIECES, r, half), sems(max(2, PIECES))]
    return st.call(kernel, [st.where] + arrays, outs, scratch, heavy=False)


def stage_split(st, choices, replicas):
    r, h = st.rows, st.hidden
    share = h // replicas
    span = PIECES * r
    arrays = listed(choices)

    def kernel(where, *refs):
        refs, rest = refs[: len(arrays)], refs[len(arrays) :]
        outs, (sb, blocks, sem) = rest[: replicas // 2], rest[replicas // 2 :]
        me = where[2]
        take_pieces(where[0], placed(choices, arrays, refs), sb, sem)
        for i in range(replicas):
            for k in range(PIECES):
                blocks[i, k * r : (k + 1) * r, :] = sb[k, :, i * share : (i + 1) * share]
        copies = []
        for q in range(replicas // 2):
            for side in range(2):
                copies.append(
                    pltpu.make_async_copy(blocks.at[me ^ (2 * q + side)], outs[q].at[side], sem.at[len(copies)])
                )
        fetch(copies)

    outs = [struct((2, span, share), BF16) for _ in range(replicas // 2)]
    scratch = [vmem(PIECES, r, h), vmem(replicas, span, share), sems(replicas)]
    return st.call(kernel, [st.where] + arrays, outs, scratch, heavy=False)


def stage_collect(st, choices):
    r, w = st.rows, st.width
    arrays = listed(choices)
    count = len(choices)

    def kernel(where, *refs):
        out, buf, sem = refs[len(arrays) :]
        take_pieces(where[0], placed(choices, arrays, refs), buf, sem)
        fetch([pltpu.make_async_copy(buf, out, sem.at[0])])

    outs = [struct((count, r, w), BF16)]
    return st.call(kernel, [st.where] + arrays, outs, [vmem(count, r, w), sems(count)], heavy=False)[0]


def stage_merge(st, parts, side=None):
    r = st.rows
    whole = side is None
    shape = parts[0].shape if whole else (r,) + parts[0].shape[2:]
    each = 1 if whole else PIECES
    count = len(parts) * each

    def kernel(*refs):
        srcs, (out, buf, sem) = refs[: len(parts)], refs[len(parts) :]
        if not whole:
            srcs = [one.at[side, pl.ds(k * r, r), :] for one in srcs for k in range(PIECES)]
        fetch([pltpu.make_async_copy(one, buf.at[i], sem.at[i]) for i, one in enumerate(srcs)])
        fetch([pltpu.make_async_copy(buf, out, sem.at[0])])

    outs = [struct((count,) + tuple(shape), BF16)]
    scratch = [vmem(count, *shape), sems(count)]
    return st.call(kernel, list(parts), outs, scratch, heavy=False)[0]


def stage_turn(st, near, near_dot, far):
    share = far.shape[2]
    r = st.rows
    count = len(near)
    span = PIECES * r

    def kernel(*refs):
        near_r, dot_r, refs = refs[:count], refs[count : 2 * count], refs[2 * count :]
        far_r, outs, (lb, ub, sem) = refs[0], refs[1 : 2 + PIECES], refs[2 + PIECES :]

        def gather(sources, first, at, size, buf):
            rows = pl.ds(at, size)
            copies = []
            for q, one in enumerate(sources):
                copies.append(pltpu.make_async_copy(one.at[0, rows, :], buf.at[pl.ds(q * size, size), :], sem.at[q]))
            for q in range(count):
                for k in range(size // r):
                    place = pl.ds((count + q) * size + k * r, r)
                    source = far_r.at[(first + q) * PIECES + at // r + k]
                    copies.append(pltpu.make_async_copy(source, buf.at[place, :], sem.at[len(copies)]))
            fetch(copies)

        for k in range(PIECES):
            gather(near_r, 0, k * r, r, lb)
            outs[k][...] = lb[...].T
        gather(dot_r, count, 0, span, ub)
        outs[PIECES][...] = ub[...].T

    outs = [struct((share, 2 * count * r), BF16) for _ in range(PIECES)] + [struct((share, 2 * count * span), BF16)]
    vm, anyspace = pl.BlockSpec(memory_space=pltpu.VMEM), pl.BlockSpec(memory_space=pl.ANY)

    def wrapped(*refs):
        kernel(*refs[: 2 * count + 1], *refs[2 * count + 2 :])

    call = pl.pallas_call(
        wrapped,
        out_shape=outs,
        in_specs=[anyspace] * (2 * count + 2),
        out_specs=[vm] * len(outs),
        scratch_shapes=[vmem(2 * count * r, share), vmem(2 * count * span, share), sems((1 + PIECES) * count)],
        compiler_params=pltpu.CompilerParams(vmem_limit_bytes=16 * 2**20),
    )
    result = call(*near, *near_dot, far, st.token)
    st.token = result[0]
    return result[:PIECES], result[PIECES]


def stage_product(st, left, rights, before, members, lanes, gram):
    share, tokens = left.shape
    w = st.width
    step = tokens // len(rights)
    vm, anyspace = pl.BlockSpec(memory_space=pltpu.VMEM), pl.BlockSpec(memory_space=pl.ANY)
    extra = ([before] if before is not None else []) + ([gram] + list(members) if members else [])

    def kernel(left_r, *refs):
        right_r, refs = refs[: len(rights)], refs[len(rights) :]
        extra_r, refs = refs[: len(extra)], refs[len(extra) + 1 :]
        if members:
            out, sums, rb, rsem, tall = refs
        else:
            out, rb, rsem = refs
        fetch(
            [
                pltpu.make_async_copy(one, rb.at[pl.ds(p * step, step), :], rsem.at[p])
                for p, one in enumerate(right_r)
            ]
        )
        value = dot_nn(left_r[...], rb[...])
        if before is not None:
            value = value + extra_r[0][...]
        out[...] = value
        if members:
            gram_r, older, prev, cur = extra_r[1:]
            size = row_block(share)
            tall[...] = jnp.zeros_like(tall)

            def run(i, carry):
                block = pl.ds(pl.multiple_of(i * size, size), size)
                mine = out[block, :]
                others = [older[j, block, :] for j in range(older.shape[0])] + [prev[block, :], cur[block, :], mine]
                for j, other in enumerate(others):
                    tall[j : j + 1, :] += jnp.sum(mine * other, axis=0, keepdims=True)
                return carry

            lax.fori_loop(0, share // size, run, 0)
            total = gram_r[...]
            for j, lane in enumerate(lanes):
                total = total + jnp.where(lane_of(lane), jnp.sum(tall[j : j + 1, :]), 0.0)
            sums[...] = total

    outs = [struct((share, w), F32)] + ([struct((1, 128), F32)] if members else [])
    call = pl.pallas_call(
        kernel,
        out_shape=outs,
        in_specs=[vm] + [anyspace] * len(rights) + [vm] * len(extra) + [anyspace],
        out_specs=[vm] * len(outs),
        scratch_shapes=[vmem(tokens, w), sems(len(rights))] + ([vmem(8, w, dtype=F32)] if members else []),
        compiler_params=pltpu.CompilerParams(vmem_limit_bytes=32 * 2**20),
    )
    result = call(left, *rights, *extra, st.token)
    st.token = result[0]
    return result


def stage_cross(st, pairs, feed, theirs):
    r, w = st.rows, st.width
    half = st.dirs.shape[0]

    def kernel(where, feed_r, theirs_r, dirs, back, mine, fb, mb, bb, sem):
        live, _ = pick(where[0], pairs)

        @pl.when(live)
        def _():
            fetch(
                [
                    pltpu.make_async_copy(theirs_r, fb.at[pl.ds(0, r), :], sem.at[0]),
                    pltpu.make_async_copy(feed_r, fb.at[pl.ds(r, r), :], sem.at[1]),
                ]
            )
            both = dot_nt(fb[...], dirs[...])
            bb[...] = both[:r].astype(BF16)
            mb[...] = both[r:]
            fetch([pltpu.make_async_copy(bb, back, sem.at[0]), pltpu.make_async_copy(mb, mine, sem.at[1])])

    outs = [struct((r, half), BF16), struct((r, half), F32)]
    scratch = [vmem(2 * r, w), vmem(r, half, dtype=F32), vmem(r, half), sems(2)]
    return st.call(kernel, [st.where, feed, theirs, st.dirs], outs, scratch, heavy=False)


def stage_curve(st, pairs, last, row_count, arrived, top, v_recv, v_mine, forwards, tangs, grads):
    r, w, h = st.rows, st.width, st.hidden
    count = len(pairs)
    half = h // 2

    def kernel(*refs):
        where, arr, top_r, vr, vm, gain, win, wout, back_r, ng_r = refs[:10]
        x_rs, pre_rs, tan_rs, pd_rs = (refs[10 + i * count : 10 + (i + 1) * count] for i in range(4))
        refs = refs[10 + 4 * count :]
        send, feed, acc, sem = refs[:4]
        gb, xb, tb, preb, pdb, backb, vb, vrb, vmb, ngb, sendb = refs[4:]
        section, upper = where[0], where[1]
        live, _ = pick(section, pairs)

        @pl.when(live)
        def _():
            takes = [
                pltpu.make_async_copy(back_r, backb, sem.at[5]),
                pltpu.make_async_copy(vr, vrb, sem.at[6]),
                pltpu.make_async_copy(vm, vmb, sem.at[7]),
                pltpu.make_async_copy(ng_r, ngb, sem.at[8]),
            ]
            sites = [s for s, _ in pairs]
            waits = [
                choose(section, list(zip(sites, x_rs)), xb, sem.at[1]),
                choose(section, list(zip(sites, tan_rs)), tb, sem.at[2]),
                choose(section, list(zip(sites, pre_rs)), preb, sem.at[3]),
                choose(section, list(zip(sites, pd_rs)), pdb, sem.at[4]),
            ]
            grad_in = pltpu.make_async_copy(arr, gb, sem.at[0])
            top_in = pltpu.make_async_copy(top_r, gb, sem.at[0])

            @pl.when(section == last)
            def _():
                top_in.start()

            @pl.when(section != last)
            def _():
                grad_in.start()

            for one in takes:
                one.start()
            grad_in.wait()

            @pl.when(section == last)
            def _():
                gb[...] = (gb[...].astype(F32) / row_count).astype(BF16)

            for one in takes:
                one.wait()
            for wait in waits:
                wait()

            @pl.when(upper == 0)
            def _():
                vb[:, :half] = vmb[...]
                vb[:, half:] = vrb[...].astype(F32)

            @pl.when(upper != 0)
            def _():
                vb[:, :half] = vrb[...].astype(F32)
                vb[:, half:] = vmb[...]

            grad_dot = gb[...]
            acc[...] = jnp.zeros_like(acc)

            def step(j, cols):
                back_dot = dot_nn(grad_dot, wout[:, cols]) + vb[:, cols]
                slope, bend = gelu_slope_bend(preb[:, cols])
                pre_grad_dot = bend * pdb[:, cols] * backb[:, cols] + slope * back_dot
                acc[...] += dot_nt(pre_grad_dot.astype(BF16), win[:, cols])

            st.sweep(step)
            tan = tb[...].astype(F32)
            x_hat, scale = standardize(xb[...].astype(F32))
            shift = tan - mean_of(tan)
            slant = mean_of(x_hat * shift)
            hat_dot = scale * (shift - x_hat * slant)
            scale_dot = -scale * scale * slant
            h_grad = ngb[...] * gain[...]
            h_dot = acc[...] * gain[...]
            along = mean_of(h_grad * x_hat)
            pull = h_grad - mean_of(h_grad) - x_hat * along
            along_dot = mean_of(h_dot * x_hat + h_grad * hat_dot)
            pull_dot = h_dot - mean_of(h_dot) - hat_dot * along - x_hat * along_dot
            move = scale_dot * pull + scale * pull_dot
            sendb[...] = (grad_dot.astype(F32) + move).astype(BF16)
            fetch(
                [
                    pltpu.make_async_copy(sendb, send, sem.at[9]),
                    pltpu.make_async_copy(gb, feed, sem.at[10]),
                ]
            )

    outs = [struct((r, w), BF16), struct((r, w), BF16)]
    scratch = st.accumulator() + [
        sems(11), vmem(r, w), vmem(r, w), vmem(r, w), vmem(r, h, dtype=F32), vmem(r, h, dtype=F32),
        vmem(r, h, dtype=F32), vmem(r, h, dtype=F32), vmem(r, half), vmem(r, half, dtype=F32),
        vmem(r, w, dtype=F32), vmem(r, w),
    ]
    arrays = [st.where, arrived, top, v_recv, v_mine, st.gain, st.w_in, st.w_out_t, grads[2], grads[3]]
    arrays += [one[1] for one in forwards] + [one[2] for one in forwards]
    arrays += [one[1] for one in tangs] + [one[2] for one in tangs]
    return st.call(kernel, arrays, outs, scratch)


def row_block(rows):
    for size in range(min(rows, 80), 0, -1):
        if rows % size == 0 and size % 8 == 0:
            return size
    return rows


def lane_of(at):
    return lax.broadcasted_iota(jnp.int32, (1, 128), 1) == at


def inner_products(st, older, prev, cur, lanes):
    rows = cur.shape[0]
    size = row_block(rows)

    def kernel(older_r, prev_r, cur_r, token, out, tall):
        tall[...] = jnp.zeros_like(tall)

        def run(i, carry):
            block = pl.ds(pl.multiple_of(i * size, size), size)
            values = [older_r[j, block, :] for j in range(older_r.shape[0])] + [prev_r[block, :], cur_r[block, :]]
            for j, (a, b) in enumerate(lanes):
                tall[j : j + 1, :] += jnp.sum(values[a] * values[b], axis=0, keepdims=True)
            return carry

        lax.fori_loop(0, rows // size, run, 0)
        total = jnp.zeros((1, 128), F32)
        for j, lane in enumerate(lanes.values()):
            total = total + jnp.where(lane_of(lane), jnp.sum(tall[j : j + 1, :]), 0.0)
        out[...] = total

    vm = pl.BlockSpec(memory_space=pltpu.VMEM)
    call = pl.pallas_call(
        kernel,
        out_shape=struct((1, 128), F32),
        in_specs=[vm] * 3 + [pl.BlockSpec(memory_space=pl.ANY)],
        out_specs=vm,
        scratch_shapes=[vmem(-(-len(lanes) // 8) * 8, cur.shape[1], dtype=F32)],
        compiler_params=pltpu.CompilerParams(vmem_limit_bytes=20 * 2**20),
    )
    st.token = call(older, prev, cur, st.token)
    return st.token


def finish(packed, beta_old, hvp, members, gram_at, cross_at, square_at, entry_count):
    rows, width = hvp.shape
    count = members[0].shape[0] + 2
    size = row_block(rows)

    def kernel(packed_r, beta_r, hvp_r, older, before, now, out, entries):
        mean = lambda lane: packed_r[0, lane] / entry_count
        gram = {key: mean(lane) for key, lane in gram_at.items()}
        cross = [mean(lane) for lane in cross_at]
        square = mean(square_at)
        g = lambda i, j: gram[min(i, j), max(i, j)]
        prev, cur = count - 2, count - 1
        old = beta_r[0]
        alpha = cross[cur] - old * g(prev, cur)
        weights = [cross[j] - old * g(prev, j) - alpha * g(cur, j) for j in range(count)]
        weights[prev] = weights[prev] + old
        weights[cur] = weights[cur] + alpha
        norm = square
        for i in range(count):
            inner = 2.0 * cross[i]
            for j in range(count):
                inner = inner - weights[j] * g(i, j)
            norm = norm - weights[i] * inner
        beta = jnp.sqrt(jnp.full((1, 128), jnp.maximum(norm, 0.0) + 1e-06, F32))
        entries[...] = jnp.where(lane_of(0), alpha, beta)
        wide = beta[:, :1]

        def run(i, carry):
            block = pl.ds(pl.multiple_of(i * size, size), size)
            value = hvp_r[block, :]
            parts = [older[j, block, :] for j in range(count - 2)] + [before[block, :], now[block, :]]
            for weight, part in zip(weights, parts):
                value = value - weight * part
            out[block, :] = value / wide
            return carry

        lax.fori_loop(0, rows // size, run, 0)

    vm = pl.BlockSpec(memory_space=pltpu.VMEM)
    sm = pl.BlockSpec(memory_space=pltpu.SMEM)
    return pl.pallas_call(
        kernel,
        out_shape=[struct((rows, width), F32), struct((1, 128), F32)],
        in_specs=[sm, sm] + [vm] * 4,
        out_specs=[vm, vm],
        compiler_params=pltpu.CompilerParams(vmem_limit_bytes=48 * 2**20),
        name="finish",
    )(packed, beta_old, hvp, *members)


def shift(value, pairs, step):
    return lax.ppermute(value, "section", [(s, s + step) for s, _ in pairs])


def tick_pairs(tick, sections, start, up):
    found = []
    for s in range(sections):
        k = tick - (s if up else sections - 1 - s)
        if 0 <= k < PIECES and s >= start:
            found.append((s, k))
    return found


def gather_pieces(block, replicas):
    found = {0: block}
    bits = [1 << i for i in range(1, replicas.bit_length() - 2)] + [1]
    for bit in bits:
        for offset in list(found):
            found[offset | bit] = lax.ppermute(found[offset], "dp", xor_pairs(replicas, bit))
    return found


def send_column(block, replicas):
    found = [block]
    for offset in range(2, replicas, 2):
        found.append(lax.ppermute(block, "dp", xor_pairs(replicas, offset)))
    return found


def trade_column(blocks, replicas):
    found = [blocks[0]]
    for q in range(1, replicas // 2):
        found.append(lax.ppermute(blocks[q], "dp", xor_pairs(replicas, 2 * q)))
    return found


def swap(block, replicas):
    return lax.ppermute(block, "dp", xor_pairs(replicas, 1))


def reduce_all(value, sections, replicas):
    for axis, count in (("dp", replicas), ("section", sections)):
        bit = 1
        while bit < count:
            value = value + lax.ppermute(value, axis, xor_pairs(count, bit))
            bit *= 2
    return value


def body(
    inputs,
    targets,
    weight_in,
    hidden_bias,
    norm_gain,
    weight_out,
    current,
    previous,
    older_basis,
    beta_before,
):
    section = lax.axis_index("section")
    replica = lax.axis_index("dp")
    sections = lax.axis_size("section")
    replicas = lax.axis_size("dp")
    last = sections - 1
    top_bit = replicas // 2
    local_rows, width = inputs.shape
    hidden = weight_in.shape[2]
    rows = local_rows // PIECES
    share = hidden // replicas
    row_count = float(local_rows * replicas)
    upper = (replica & top_bit) != 0
    numbers = [section, upper, replica, replica & (top_bit - 1)]
    where = jnp.stack([one.astype(jnp.int32) for one in numbers])
    st = Stage(rows, width, hidden, where, weight_in[0], weight_out[0].T, norm_gain)
    feed = inputs.reshape(PIECES, rows, width)
    goal = targets.reshape(PIECES, rows, width)
    partner = xor_pairs(replicas, top_bit)
    both_axes = ("section", "dp")

    def cross_pairs(pairs):
        return [
            (s * replicas + i, s * replicas + (i ^ top_bit)) for s, _ in pairs for i in range(replicas)
        ]

    own_direction = current[0].astype(BF16)
    pieces = gather_pieces(own_direction, replicas)
    if share % 16:
        held = jnp.stack([pieces[offset] for offset in sorted(pieces)])
        order = (replica & (top_bit - 1)) ^ jnp.arange(top_bit)
        pieces = {0: held[order].reshape(-1, width)}

    forwards, arrived = [], feed[0]
    tops = {}
    for tick in range(sections + PIECES - 1):
        pairs = tick_pairs(tick, sections, 0, True)
        extra = () if tick else (goal, own_direction)
        forward = stage_forward(st, pairs, feed, arrived, hidden_bias, tick == 0, extra)
        forwards.append(forward)
        if tick >= last:
            tops[tick - last] = forward[0]
        going = [(s, k) for s, k in pairs if s < last]
        if going:
            arrived = shift(forward[0], going, 1)
    everywhere = range(sections)
    hid_of = [[(s, forwards[s + k][3]) for s in everywhere] for k in range(PIECES)]
    hid_mine, hid_out = stage_halves(st, hid_of)

    hid_theirs = lax.ppermute(hid_out, "dp", partner)

    g_arr = feed[0]
    crossed = []

    def run_gradient(tick):
        nonlocal g_arr
        pairs = tick_pairs(tick, sections, 1, False)
        top = tops.get(tick, g_arr)
        grads = stage_gradient(st, pairs, last, row_count, g_arr, top, goal, [forwards[s + k] for s, k in pairs])
        going = [(s, k) for s, k in pairs if s > 1]
        if going:
            g_arr = shift(grads[0], going, -1)
        theirs = lax.ppermute(grads[1], both_axes, cross_pairs(pairs))
        crossed.append((pairs, grads, theirs))

    v_terms = {}

    def run_cross(tick):
        pairs, held, theirs = crossed[tick]
        back, mine = stage_cross(st, pairs, held[1], theirs)
        came = lax.ppermute(back, both_axes, cross_pairs(pairs))
        v_terms[tick] = (came, mine)

    run_gradient(0)
    u_theirs, u_mine = stage_direction(st, pieces, hid_theirs, hid_mine)
    u_first, u_recv = [], []
    for i in range(PIECES):
        u_first.append(lax.ppermute(u_theirs[i], both_axes, cross_pairs([(0, i)])))
        rest = [(s, i) for s in range(1, sections)]
        u_recv.append(lax.ppermute(u_theirs[i], both_axes, cross_pairs(rest)))
    from_first = []

    def run_first(i):
        from_first.append(shift(stage_first(st, u_mine, u_first[i], i), [(0, 0)], 1))

    tangs, t_arr = {}, feed[0]
    t_tops = {}

    def run_tangent(tick):
        nonlocal t_arr
        pairs = tick_pairs(tick, sections, 1, True)
        came = from_first[min(tick - 1, PIECES - 1)]
        held = [u_recv[max(k for _, k in pairs) if i else 0] for i in range(2)]
        tang = stage_tangent(st, pairs, came, t_arr, u_mine, held, forwards[tick])
        tangs[tick] = tang
        if tick >= last:
            t_tops[tick - last] = tang[0]
        going = [(s, k) for s, k in pairs if s < last]
        if going:
            t_arr = shift(tang[0], going, 1)

    curves, d_arr = [], feed[0]
    tail = {}

    def run_curve(tick):
        nonlocal d_arr
        pairs = tick_pairs(tick, sections, 1, False)
        top = t_tops.get(tick, d_arr)
        v_recv, v_mine = v_terms[tick]
        curve = stage_curve(
            st, pairs, last, row_count, d_arr, top, v_recv, v_mine,
            [forwards[s + k] for s, k in pairs], [tangs[s + k] for s, k in pairs], crossed[tick][1],
        )
        curves.append(curve)
        d_arr = shift(curve[0], pairs, -1)
        for s, k in pairs:
            if s == 1:
                tail[k] = d_arr

    older = older_basis[:, 0]
    members = [older, previous[0], current[0]]
    count = older.shape[0] + 2
    keys = [(i, j) for i in range(count) for j in range(i, count)]
    gram_at = {key: lane for lane, key in enumerate(keys)}
    cross_at = [len(keys) + i for i in range(count)]
    square_at = len(keys) + count

    run_gradient(1)
    run_first(0)
    run_cross(0)
    run_tangent(1)
    run_first(1)
    run_tangent(2)
    near = trade_column(stage_split(st, hid_of, replicas), replicas)
    run_cross(1)
    run_tangent(3)
    run_gradient(2)
    run_curve(0)
    run_tangent(4)
    later = range(1, sections)
    dot_of = [[(s, tangs[s + k][3]) for s in later] for k in range(PIECES)]
    near_dot = trade_column(stage_split(st, dot_of, replicas), replicas)
    run_curve(1)
    run_cross(2)
    run_gradient(3)
    run_cross(3)
    grad_of = [[(s, crossed[last - s + k][1][1]) for s in later] for k in range(PIECES)]
    grad_column = send_column(stage_collect(st, grad_of), replicas)
    run_curve(2)
    columns = []

    def run_tail(i):
        options = [(0, tail[i])] + [(s, curves[last - s + i][1]) for s in later]
        block = stage_collect(st, [options])[0]
        columns.append(send_column(block, replicas))

    run_tail(0)
    run_curve(3)
    far = swap(stage_merge(st, near + near_dot, 1), replicas)
    run_tail(1)
    grad_near = stage_merge(st, grad_column)
    grad_far = swap(grad_near, replicas)
    flat = lambda one: one.reshape(-1, width)
    hid_turned, slope_turned = stage_turn(st, near, near_dot, far)
    gram = inner_products(st, *members, gram_at)
    nears = [stage_merge(st, columns[0])]
    fars = [swap(nears[0], replicas)]
    total = stage_product(st, slope_turned, [flat(grad_near), flat(grad_far)], None, None, None, None)[0]
    for k in range(PIECES):
        if k > 0:
            nears.append(stage_merge(st, columns[k]))
            fars.append(swap(nears[k], replicas))
        ending = (members, cross_at + [square_at], gram) if k == PIECES - 1 else (None, None, None)
        product = stage_product(st, hid_turned[k], [flat(nears[k]), flat(fars[k])], total, *ending)
        total = product[0]
    hvp, local = product

    entry_count = float(share * width * sections * replicas)
    packed = reduce_all(local, sections, replicas)
    vector, entries = finish(
        packed, beta_before, hvp, members, gram_at, cross_at, square_at, entry_count
    )
    return (vector[None], entries[0, :2])


def solution(mesh):
    return jax.shard_map(
        body,
        mesh=mesh,
        in_specs=(
            P("dp", None),
            P("dp", None),
            P("section", None, None),
            P("section", None),
            P("section", None),
            P("section", None, None),
            P("section", "dp", None),
            P("section", "dp", None),
            P(None, "section", "dp", None),
            P(),
        ),
        out_specs=(P("section", "dp", None), P()),
        check_vma=False,
    )
```
